32 devices in a mesh: groups: 2 (over x), ctx: 16 (over z, y, core).
Axes of the slice: x: 2, y: 2, z: 4, core: 2. Of those that a mesh axis runs over, the one named last changes fastest.
Arguments:
- queries: bfloat16 [8192, 4096], P(('groups', 'ctx')), parts along dimension 0, may hold values from -160 to 160
- keys: bfloat16 [8192, 512], P(('groups', 'ctx')), parts along dimension 0, may hold values from -6 to 6
- values: bfloat16 [8192, 512], P(('groups', 'ctx')), parts along dimension 0, may hold values from -6 to 6
- doc_flags: int32 [64], P(('groups', 'ctx')), parts along dimension 0, may hold values from 0 to 1, as said below
Outputs:
- attention: bfloat16 [8192, 4096], P(('groups', 'ctx')), parts along dimension 0
The draws below stay inside these ranges and needn't reach their ends.
There are 2 independent parts, one for each index of `groups`. The reference program is written for one: setup_inputs(seed, part) draws one part's arguments, and reference() takes and returns one part's arrays. A program takes and returns all parts, laid end to end along the dimension named above; each array names one. Nothing has to cross between parts.
Inputs may be any that keep to these rules, and one draw needn't show every extreme that they name: `doc_flags`: block 0 starts a document; every document spans 1 to 6 blocks and one spans exactly 6 blocks.
All inputs are finite; a program needn't handle non-finite values.
Results may differ from the reference program's by a relative error of at most 0.0039.
Values may be sent and summed in bfloat16 or wider, within the bound.
A program may use at most 64 MiB of HBM per device.

```python
import jax
import jax.numpy as jnp
from jax import lax

HD = 128
KVH = 4
GROUP = 8
BLK = 128
ROUNDS = 4
TOK_DEV = 256
H = 32
TOKENS = 4096
NBLK = 32
MOST_BLK = 6
N_CTX = 16


def paired_draw(key):
    key_query, key_keys = jax.random.split(jax.random.fold_in(key, 7), 2)
    key_rows = jnp.clip(jax.random.normal(key_keys, (TOKENS, KVH * HD), jnp.float32), -6.0, 6.0)
    query_rows = jnp.clip(jax.random.normal(key_query, (TOKENS, H * HD), jnp.float32), -6.0, 6.0)
    return (query_rows, key_rows)


def draw_queries(key, part):
    return paired_draw(key)[0].astype(jnp.bfloat16)


def draw_keys(key, part):
    return paired_draw(key)[1].astype(jnp.bfloat16)


def draw_doc_flags(key, part):
    key_lengths, key_spot = jax.random.split(jax.random.fold_in(key, 11))
    lengths = jax.random.randint(key_lengths, (NBLK,), 1, MOST_BLK + 1)
    spot = jax.random.randint(key_spot, (), 0, NBLK // MOST_BLK)
    lengths = jnp.where(jnp.arange(NBLK) == spot, MOST_BLK, lengths).astype(jnp.int32)
    starts = jnp.cumsum(lengths).astype(jnp.int32) - lengths
    hits = jnp.arange(NBLK, dtype=jnp.int32)[:, None] == starts[None, :]
    return jnp.any(hits, axis=1).astype(jnp.int32)


def block_scale(key, extent, shards, low, largest):
    def one(dim, shards_of):
        steps = jax.random.uniform(jax.random.fold_in(jax.random.fold_in(key, 6), dim), (shards_of,), jnp.float32, low / len(shards), largest / len(shards))
        return jnp.repeat(jnp.exp(steps), extent[dim] // shards_of).reshape((-1,) + (1,) * (len(extent) - dim - 1))

    factor_of = one(*shards[0])
    for cut in shards[1:]:
        factor_of = factor_of * one(*cut)
    return factor_of


def normal_values(key, shape, scale, most, cuts=(), kind=jnp.bfloat16):
    drawn = scale * jax.random.normal(key, shape, jnp.float32)
    if cuts:
        drawn = drawn * block_scale(key, shape, cuts, -0.22, 0.18)
    return jnp.clip(drawn, -most, most).astype(kind)


def setup_inputs(seed: int = 0, part: int = 0) -> dict:
    seeds = jax.random.split(jax.random.key(seed), 5)
    part_splits = jax.random.split(jax.random.fold_in(seeds[4], part), 5)
    queries = draw_queries(jax.random.fold_in(jax.random.fold_in(seeds[4], part), 71), part)
    keys = draw_keys(jax.random.fold_in(jax.random.fold_in(seeds[4], part), 71), part)
    values = normal_values(part_splits[2], (TOKENS, KVH * HD), 1.0, 6.0, ((0, 16),))
    doc_flags = draw_doc_flags(jax.random.fold_in(jax.random.fold_in(seeds[4], part), 71), part)
    return {"queries": queries, "keys": keys, "values": values, "doc_flags": doc_flags}


NEG_FILL = -1.0e30


def reference(queries, keys, values, doc_flags):
    rows = TOK_DEV
    reach = ROUNDS * TOK_DEV
    lead = (ROUNDS - 1) * TOK_DEV
    scale = 1.0 / (HD ** 0.5)
    token_doc = jnp.repeat(jnp.cumsum(doc_flags).astype(jnp.int32), BLK, total_repeat_length=TOKENS)
    padded_doc = jnp.concatenate([jnp.full((lead,), -1, jnp.int32), token_doc])
    padded_keys = jnp.concatenate([jnp.zeros((lead, KVH * HD), keys.dtype), keys])
    padded_values = jnp.concatenate([jnp.zeros((lead, KVH * HD), values.dtype), values])

    def one_stretch(stretch):
        start = (stretch * rows).astype(jnp.int32)
        q_rows = lax.dynamic_slice_in_dim(queries, start, rows, 0)
        k_rows = lax.dynamic_slice_in_dim(padded_keys, start, reach, 0)
        v_rows = lax.dynamic_slice_in_dim(padded_values, start, reach, 0)
        doc_keys = lax.dynamic_slice_in_dim(padded_doc, start, reach, 0)
        doc_query = lax.dynamic_slice_in_dim(token_doc, start, rows, 0)
        query_pos = start + jnp.arange(rows, dtype=jnp.int32)
        key_pos = start - lead + jnp.arange(reach, dtype=jnp.int32)
        allowed = (key_pos[None, :] >= 0) & (key_pos[None, :] <= query_pos[:, None]) & (doc_keys[None, :] == doc_query[:, None])
        pieces = []
        for group in range(KVH):
            q_group = q_rows[:, group * GROUP * HD:(group + 1) * GROUP * HD].reshape(rows, GROUP, HD).astype(jnp.float32)
            k_group = k_rows[:, group * HD:(group + 1) * HD].astype(jnp.float32)
            v_group = v_rows[:, group * HD:(group + 1) * HD].astype(jnp.float32)
            scored = jnp.einsum('sjd,td->jst', q_group, k_group, precision=lax.Precision.HIGHEST) * scale
            scored = jnp.where(allowed[None], scored, NEG_FILL)
            top = jnp.max(scored, axis=2, keepdims=True)
            weights = jnp.exp(scored - top)
            total = jnp.sum(weights, axis=2)
            rounded = lax.optimization_barrier(weights.astype(jnp.bfloat16))
            mixed = jnp.einsum('jst,td->sjd', rounded.astype(jnp.float32), v_group, precision=lax.Precision.HIGHEST)
            pieces.append((mixed / total.T[:, :, None]).astype(jnp.bfloat16).reshape(rows, GROUP * HD))
        return jnp.concatenate(pieces, axis=1)

    stretches = lax.map(one_stretch, jnp.arange(N_CTX, dtype=jnp.int32))
    return stretches.reshape(TOKENS, H * HD)
```

```python
import functools
import math

import jax
import jax.numpy as jnp
from jax import lax
from jax.experimental import pallas as pl
from jax.experimental.pallas import tpu as pltpu
from jax.sharding import PartitionSpec as P

HD = 128
KVH = 4
GROUP = 8
BLK = 128
BACK = 5
NEG_FILL = -1e30
SCALE2 = math.log2(math.e) / math.sqrt(HD)
MESH = pl.DeviceIdType.MESH
LAST = KVH - 1
RELAYED = (2, 3)

ROWS = {3: (0, BLK), 2: (BLK, 2 * BLK), 1: (3 * BLK, 2 * BLK), 0: (5 * BLK, 2 * BLK)}
WINDOW = 7 * BLK
REACH = 6 * BLK

HEADS = [pl.ds(j * HD, HD) for j in range(GROUP)]


def score(i, q_ref, k_ref, bias):
    rows, keys = pl.ds(i * BLK, BLK), pl.ds(i * BLK, REACH)
    key_at = lax.broadcasted_iota(jnp.int32, (BLK, BLK), 0)
    row_at = lax.broadcasted_iota(jnp.int32, (BLK, BLK), 1)
    eye = (key_at == row_at).astype(jnp.bfloat16)
    q = jnp.concatenate(
        [jnp.concatenate([q_ref[rows, head], eye], axis=1) for head in HEADS], axis=0
    )
    k = jnp.concatenate([k_ref[keys, :], bias[i]], axis=1)
    return lax.dot_general(q, k, (((1,), (1,)), ((), ())), preferred_element_type=jnp.float32)


def weigh(s):
    top = jnp.max(s, axis=1, keepdims=True) * SCALE2
    return jnp.exp2(s * SCALE2 - top).astype(jnp.bfloat16)


def mix(i, w, v_ref, o_ref):
    rows, keys = pl.ds(i * BLK, BLK), pl.ds(i * BLK, REACH)
    v = jnp.concatenate([v_ref[keys, :], jnp.ones((REACH, HD), jnp.bfloat16)], axis=1)
    mixed = jnp.dot(w, v, preferred_element_type=jnp.float32)
    out = (mixed[:, :HD] / mixed[:, HD:]).astype(jnp.bfloat16)
    for j, head in enumerate(HEADS):
        o_ref[rows, head] = out[j * BLK:(j + 1) * BLK]


def last_kernel(o_first, v_win, w_last, o_hbm, o_buf, sem):
    width = GROUP * HD
    moves = []
    for g in range(LAST):
        move = pltpu.make_async_copy(
            o_first.at[g], o_hbm.at[:, pl.ds(g * width, width)], sem.at[g]
        )
        move.start()
        moves.append(move)
    for i in range(2):
        mix(i, w_last[i], v_win.at[LAST], o_buf)
        rows = pl.ds(i * BLK, BLK)
        move = pltpu.make_async_copy(
            o_buf.at[rows, :], o_hbm.at[rows, pl.ds(LAST * width, width)], sem.at[LAST + i]
        )
        move.start()
        moves.append(move)
    for move in moves:
        move.wait()


def kernel(
    n, relayed, q_hbm, k_hbm, v_hbm, flags_hbm,
    o_buf, v_win, w_last,
    q_buf, k_win, bias, s_buf, passing, flags_ref, flags_out, flags_in,
    q_sem, own_sem, flag_sem, main_send, main_recv, side_send, side_recv,
    near_send, near_recv, half_send, half_recv, pass_send, pass_recv,
    fsend_sem, frecv_sem, ready,
):
    me = lax.axis_index("ctx")
    even, odd = lax.rem(me, 2) == 0, lax.rem(me, 2) == 1
    prev, prev2 = me >= 2, me >= 4
    after, after2 = me + 2 < n, me + 4 < n
    hands = (lax.rem(me, 4) == 3) & after
    passes = (lax.rem(me, 4) == 1) & (me + 4 < n)
    takes = (lax.rem(me, 4) == 1) & (me >= 4)

    wins, hbms = (k_win, v_win), (k_hbm, v_hbm)

    def columns(g):
        return pl.ds(pl.multiple_of(g * HD, HD), HD)

    def window(kv, g, back):
        start, size = ROWS[back]
        return wins[kv].at[g, pl.ds(start, size), :]

    def own(g, kv, first=0, rows=2 * BLK):
        return hbms[kv].at[pl.ds(first, rows), columns(g)]

    def q_copy(g):
        cols = pl.ds(pl.multiple_of(g * GROUP * HD, GROUP * HD), GROUP * HD)
        return pltpu.make_async_copy(q_hbm.at[:, cols], q_buf.at[g], q_sem.at[g])

    def own_copy(g, kv):
        return pltpu.make_async_copy(own(g, kv), window(kv, g, 0), own_sem.at[g, kv])

    def remote(src, dst, send, recv, to):
        return pltpu.make_async_remote_copy(
            src_ref=src, dst_ref=dst, send_sem=send, recv_sem=recv,
            device_id={"ctx": to}, device_id_type=MESH,
        )

    def odd_main(g, kv):
        return remote(own(g, kv), window(kv, g, 2), main_send.at[g, kv], main_recv.at[g, kv], me + 2)

    def even_main(g, kv):
        return remote(
            own(g, kv, BLK, BLK), window(kv, g, 3), half_send.at[g, kv], half_recv.at[g, kv], me + 3
        )

    def even_side(g, kv):
        return remote(
            own(g, kv, 0, BLK), wins[kv].at[g, pl.ds(BLK, BLK), :],
            main_send.at[g, kv], main_recv.at[g, kv], me + 2,
        )

    def odd_side(g, kv):
        return remote(
            own(g, kv, BLK, BLK), window(kv, g, 3), side_send.at[g, kv], side_recv.at[g, kv], me + 3
        )

    def even_near(g, kv):
        return remote(own(g, kv), window(kv, g, 1), near_send.at[g, kv], near_recv.at[g, kv], me + 1)

    def odd_near(g, kv):
        return remote(
            window(kv, g, 2), window(kv, g, 1), near_send.at[g, kv], near_recv.at[g, kv], me - 1
        )

    def odd_half(g, kv):
        return remote(
            window(kv, g, 3), wins[kv].at[g, pl.ds(2 * BLK, BLK), :],
            half_send.at[g, kv], half_recv.at[g, kv], me - 1,
        )

    def hand(at, kv):
        g = relayed[0] + at
        return remote(
            own(g, kv), passing.at[at, kv], main_send.at[g, kv], pass_recv.at[at, kv], me - 2
        )

    def passed(at, kv):
        g = relayed[0] + at
        return remote(
            passing.at[at, kv], window(kv, g, 2), pass_send.at[at, kv], main_recv.at[g, kv], me + 4
        )

    def flag_same():
        return remote(flags_out, flags_in.at[1], fsend_sem.at[0], frecv_sem.at[1], me + 2)

    def flag_even():
        return remote(flags_out, flags_in.at[0], fsend_sem.at[1], frecv_sem.at[0], me + 1)

    def flag_odd():
        return remote(flags_in.at[1], flags_in.at[0], fsend_sem.at[1], frecv_sem.at[0], me - 1)

    flag_copy = pltpu.make_async_copy(flags_hbm, flags_ref, flag_sem)
    flag_copy.start()
    barrier = pltpu.get_barrier_semaphore()

    greet = [
        (odd, -1), (odd & prev, -2), (odd & prev, -3), (odd & after2, 3), (even & after, 2),
    ]
    heard = [(even, 1), (odd & after, 1), (even & after, 1), (even & prev2, 1), (even & prev, 1)]
    if relayed:
        greet += [(passes, 2), (takes, -4)]
        heard += [(hands, 1), (passes, 1)]
    for there, step in greet:
        @pl.when(there)
        def _():
            pl.semaphore_signal(barrier, inc=1, device_id={"ctx": me + step}, device_id_type=MESH)

    for g in range(KVH):
        for kv in range(2):
            own_copy(g, kv).start()
        q_copy(g).start()
    flag_copy.wait()
    flags_out[0:1, :] = jnp.full((1, BLK), flags_ref[0], jnp.int32)
    flags_out[1:2, :] = jnp.full((1, BLK), flags_ref[1], jnp.int32)
    flags_out[2:8, :] = jnp.zeros((6, BLK), jnp.int32)

    def blank(there, back):
        @pl.when(there)
        def _():
            start, size = ROWS[back]
            for win in wins:
                win[:, start:start + size, :] = jnp.zeros((KVH, size, HD), jnp.bfloat16)
            if back < 3:
                flags_in[back - 1] = jnp.zeros((8, BLK), jnp.int32)

    first = jnp.logical_not(prev)
    blank(even & first, 1)
    blank(first, 2)
    blank(odd & first | even & jnp.logical_not(prev2), 3)

    count = jnp.int32(0)
    for there, amount in heard:
        count = count + jnp.where(there, amount, 0)

    @pl.when(even | after)
    def _():
        pl.semaphore_wait(barrier, count)

    def signal(there, at, step):
        @pl.when(there)
        def _():
            pl.semaphore_signal(
                ready.at[at], inc=1, device_id={"ctx": me + step}, device_id_type=MESH
            )

    pieces = [(g, kv) for g in range(KVH) for kv in range(2)]

    signal(even, 0, 1)
    signal(even & prev, 0, -2)
    signal(even & prev2, 1, -3)

    def forward(g, kv):
        @pl.when(odd & prev)
        def _():
            odd_main(g, kv).wait_recv()
            odd_near(g, kv).start()
            even_main(g, kv).wait_recv()
            odd_half(g, kv).start()

    def arrive(g, kv):
        forward(g, kv)

        @pl.when(odd)
        def _():
            even_near(g, kv).wait_recv()

        @pl.when(even & prev)
        def _():
            odd_near(g, kv).wait_recv()
            odd_half(g, kv).wait_recv()
            even_side(g, kv).wait_recv()

        @pl.when(even & prev2)
        def _():
            odd_side(g, kv).wait_recv()

        own_copy(g, kv).wait()
        if kv == 0:
            q_copy(g).wait()

    def pass_on(at, kv):
        if relayed:
            @pl.when(passes & (at < len(relayed)))
            def _():
                hand(at, kv).wait_recv()
                passed(at, kv).start()

    @pl.when(odd & after)
    def _():
        flag_same().start()

    for g, kv in pieces:
        if g in relayed:
            @pl.when(hands)
            def _():
                hand(g - relayed[0], kv).start()

            @pl.when(odd & after & jnp.logical_not(hands))
            def _():
                odd_main(g, kv).start()
        else:
            @pl.when(odd & after)
            def _():
                odd_main(g, kv).start()

    @pl.when(even & after)
    def _():
        even_main(0, 0).start()

    @pl.when(even)
    def _():
        flag_even().start()
        for g, kv in pieces:
            even_near(g, kv).start()

    @pl.when(even & after)
    def _():
        pl.semaphore_wait(ready.at[0], 1)
        flag_same().start()
        for g, kv in pieces:
            if (g, kv) != (0, 0):
                even_main(g, kv).start()
            even_side(g, kv).start()

    @pl.when(odd)
    def _():
        pl.semaphore_wait(ready.at[0], 1)

    @pl.when(odd & prev)
    def _():
        flag_same().wait_recv()
        flag_odd().start()

    @pl.when(odd & after2)
    def _():
        pl.semaphore_wait(ready.at[1], 1)
        for g, kv in pieces:
            odd_side(g, kv).start()

    @pl.when(odd)
    def _():
        flag_even().wait_recv()

    @pl.when(even & prev)
    def _():
        flag_odd().wait_recv()
        flag_same().wait_recv()

    mine = flags_out[...]
    begins = {0: mine[0:1], 1: mine[1:2]}
    for back in (1, 2):
        got = flags_in[back - 1]
        begins[-2 * back], begins[1 - 2 * back] = got[0:1], got[1:2]
    key_at = lax.broadcasted_iota(jnp.int32, (BLK, BLK), 0)
    row_at = lax.broadcasted_iota(jnp.int32, (BLK, BLK), 1)
    causal = jnp.where(key_at <= row_at, 0.0, NEG_FILL).astype(jnp.bfloat16)
    for i in range(2):
        bias[i, BACK * BLK:(BACK + 1) * BLK, :] = causal
        hidden = jnp.zeros((1, BLK), jnp.float32)
        for b in range(i - 1, i - BACK - 1, -1):
            hidden = jnp.where(begins[b + 1] != 0, NEG_FILL, hidden)
            at = (b - i + BACK) * BLK
            bias[i, at:at + BLK, :] = jnp.broadcast_to(hidden, (BLK, BLK)).astype(jnp.bfloat16)

    arrive(0, 0)
    s_buf[0] = score(0, q_buf.at[0], k_win.at[0], bias)

    def one_group(g, carry):
        arrive(g, 1)
        pass_on(g, 0)
        s_buf[1] = score(1, q_buf.at[g], k_win.at[g], bias)
        mix(0, weigh(s_buf[0]), v_win.at[g], o_buf.at[g])
        arrive(g + 1, 0)
        pass_on(g, 1)
        s_buf[0] = score(0, q_buf.at[g + 1], k_win.at[g + 1], bias)
        mix(1, weigh(s_buf[1]), v_win.at[g], o_buf.at[g])
        return carry

    lax.fori_loop(0, LAST, one_group, 0)
    s_buf[1] = score(1, q_buf.at[LAST], k_win.at[LAST], bias)
    w_last[0] = weigh(s_buf[0])
    w_last[1] = weigh(s_buf[1])
    arrive(LAST, 1)

    def drained(there, copies):
        @pl.when(there)
        def _():
            for copy in copies:
                copy().wait_send()

    drained(after, [flag_same])
    drained(even, [flag_even])
    drained(odd & prev, [flag_odd])

    def drain(g, carry):
        for kv in range(2):
            @pl.when(odd & after)
            def _():
                odd_main(g, kv).wait_send()

            @pl.when(odd & after2)
            def _():
                odd_side(g, kv).wait_send()

            @pl.when(odd & prev)
            def _():
                odd_near(g, kv).wait_send()
                odd_half(g, kv).wait_send()

            @pl.when(even & after)
            def _():
                even_main(g, kv).wait_send()
                even_side(g, kv).wait_send()

            @pl.when(even)
            def _():
                even_near(g, kv).wait_send()
        return carry

    lax.fori_loop(0, KVH, drain, 0)
    for at in range(len(relayed)):
        @pl.when(passes)
        def _():
            for kv in range(2):
                passed(at, kv).wait_send()


def per_device(n, relayed, queries, keys, values, doc_flags):
    rows = queries.shape[0]
    dma = pltpu.SemaphoreType.DMA
    inputs = [
        pltpu.with_memory_space_constraint(x, pltpu.HBM)
        for x in (queries, keys, values, doc_flags)
    ]
    kept = max(1, len(relayed))
    staged = pl.pallas_call(
        functools.partial(kernel, n, relayed),
        out_shape=[
            pltpu.VMEM((LAST, rows, GROUP * HD), jnp.bfloat16),
            pltpu.VMEM((KVH, WINDOW, HD), jnp.bfloat16),
            pltpu.VMEM((2, GROUP * BLK, REACH), jnp.bfloat16),
        ],
        in_specs=[pl.BlockSpec(memory_space=pltpu.HBM)] * 4,
        out_specs=[pl.BlockSpec(memory_space=pltpu.VMEM)] * 3,
        scratch_shapes=[
            pltpu.VMEM((KVH, rows, GROUP * HD), jnp.bfloat16),
            pltpu.VMEM((KVH, WINDOW, HD), jnp.bfloat16),
            pltpu.VMEM((2, REACH, BLK), jnp.bfloat16),
            pltpu.VMEM((2, GROUP * BLK, REACH), jnp.float32),
            pltpu.VMEM((kept, 2, rows, HD), jnp.bfloat16),
            pltpu.SMEM(doc_flags.shape, jnp.int32),
            pltpu.VMEM((8, BLK), jnp.int32),
            pltpu.VMEM((2, 8, BLK), jnp.int32),
            dma((KVH,)),
            dma((KVH, 2)),
            dma,
            dma((KVH, 2)),
            dma((KVH, 2)),
            dma((KVH, 2)),
            dma((KVH, 2)),
            dma((KVH, 2)),
            dma((KVH, 2)),
            dma((KVH, 2)),
            dma((KVH, 2)),
            dma((kept, 2)),
            dma((kept, 2)),
            dma((2,)),
            dma((2,)),
            pltpu.SemaphoreType.REGULAR((2,)),
        ],
        compiler_params=pltpu.CompilerParams(
            collective_id=0, has_side_effects=True, vmem_limit_bytes=40 * 1024 * 1024
        ),
        name="window_attention",
    )(*inputs)
    return pl.pallas_call(
        last_kernel,
        out_shape=jax.ShapeDtypeStruct(queries.shape, jnp.bfloat16),
        in_specs=[pl.BlockSpec(memory_space=pltpu.VMEM)] * 3,
        out_specs=pl.BlockSpec(memory_space=pltpu.HBM),
        scratch_shapes=[pltpu.VMEM((rows, GROUP * HD), jnp.bfloat16), dma((KVH + 1,))],
        compiler_params=pltpu.CompilerParams(vmem_limit_bytes=32 * 1024 * 1024),
        name="last_group",
    )(*staged)


def solution(mesh):
    spread = P(("groups", "ctx"), None)
    n = mesh.shape["ctx"]
    relayed = RELAYED if mesh.shape["groups"] == 2 else ()
    return jax.shard_map(
        functools.partial(per_device, n, relayed),
        mesh=mesh,
        in_specs=(spread, spread, spread, P(("groups", "ctx"))),
        out_specs=spread,
        check_vma=False,
    )
```

```python
import functools
import math

import jax
import jax.numpy as jnp
from jax import lax
from jax.experimental import pallas as pl
from jax.experimental.pallas import tpu as pltpu
from jax.sharding import PartitionSpec as P

HD = 128
KVH = 4
GROUP = 8
BLK = 128
BACK = 5
NEG_FILL = -1e30
SCALE2 = math.log2(math.e) / math.sqrt(HD)
MESH = pl.DeviceIdType.MESH
LAST = KVH - 1
PIECES = [(g, kv) for g in range(KVH) for kv in range(2)]
RELAYED = [(LAST, 1)]
LATE = 4
PASS_AT = 1
SEMS = 9
ODD_LEAD = 2
EVEN_LEAD = 1

ROWS = {3: (0, BLK), 2: (BLK, 2 * BLK), 1: (3 * BLK, 2 * BLK), 0: (5 * BLK, 2 * BLK)}
WINDOW = 7 * BLK
REACH = 6 * BLK

HEADS = [pl.ds(j * HD, HD) for j in range(GROUP)]
STEP = 4
PARTS = [
    (pl.ds(j * BLK, STEP * BLK), HEADS[j:j + STEP]) for j in range(0, GROUP, STEP)
]


def score(i, q_ref, k_ref, bias, heads=HEADS):
    rows, keys = pl.ds(i * BLK, BLK), pl.ds(i * BLK, REACH)
    key_at = lax.broadcasted_iota(jnp.int32, (BLK, BLK), 0)
    row_at = lax.broadcasted_iota(jnp.int32, (BLK, BLK), 1)
    eye = (key_at == row_at).astype(jnp.bfloat16)
    q = jnp.concatenate(
        [jnp.concatenate([q_ref[rows, head], eye], axis=1) for head in heads], axis=0
    )
    k = jnp.concatenate([k_ref[keys, :], bias[i]], axis=1)
    return lax.dot_general(q, k, (((1,), (1,)), ((), ())), preferred_element_type=jnp.float32)


def weigh(s):
    top = jnp.max(s, axis=1, keepdims=True) * SCALE2
    return jnp.exp2(s * SCALE2 - top).astype(jnp.bfloat16)


def mix(i, w, v_ref, o_ref, heads=HEADS):
    v = jnp.concatenate(
        [v_ref[pl.ds(i * BLK, REACH), :], jnp.ones((REACH, HD), jnp.bfloat16)], axis=1
    )
    both = jnp.dot(w, v, preferred_element_type=jnp.float32)
    out = (both[:, :HD] / both[:, HD:]).astype(jnp.bfloat16)
    for j, head in enumerate(heads):
        o_ref[pl.ds(i * BLK, BLK), head] = out[j * BLK:(j + 1) * BLK]


def weigh_and_mix(s_ref, w_ref, i, mix_ref, v_ref, o_ref):
    for rows, heads in PARTS:
        w_ref[rows, :] = weigh(s_ref[rows, :])
        mix(i, mix_ref[rows, :], v_ref, o_ref, heads)


def last_kernel(o_first, v_win, w_last, s_last, o_hbm, o_buf, w_first, sem):
    width = GROUP * HD
    moves = []
    for g in range(LAST):
        move = pltpu.make_async_copy(
            o_first.at[g], o_hbm.at[:, pl.ds(g * width, width)], sem.at[g]
        )
        move.start()
        moves.append(move)
    for i in (1, 0):
        if i:
            weigh_and_mix(s_last.at[0], w_first, 1, w_last, v_win.at[LAST], o_buf)
        else:
            mix(0, w_first[...], v_win.at[LAST], o_buf)
        rows = pl.ds(i * BLK, BLK)
        move = pltpu.make_async_copy(
            o_buf.at[rows, :], o_hbm.at[rows, pl.ds(LAST * width, width)], sem.at[LAST + i]
        )
        move.start()
        moves.append(move)
    for move in moves:
        move.wait()


def kernel(
    n, relayed, q_hbm, k_hbm, v_hbm, flags_hbm,
    o_buf, v_win, w_last, s_buf,
    q_buf, k_win, bias, passing, flags_ref, flags_out, flags_in,
    sem, main_recv, half_recv, side_recv, pass_recv, flag_recv, ready,
):
    me = lax.axis_index("ctx")
    even, odd = lax.rem(me, 2) == 0, lax.rem(me, 2) == 1
    place = lax.rem(me, 4)
    prev, prev2 = me >= 2, me >= 4
    after, after2 = me + 2 < n, me + 4 < n
    hands = (place == 3) & after & bool(relayed)
    passes = (place == 1) & after2 & bool(relayed)

    wins, hbms = (k_win, v_win), (k_hbm, v_hbm)
    q_sem, own_sem, flag_sem, main_send, side_send, near_send, pass_send, near_flag, far_flag = (
        sem.at[at] for at in range(SEMS)
    )

    def columns(g):
        return pl.ds(pl.multiple_of(g * HD, HD), HD)

    def window(kv, g, back):
        start, size = ROWS[back]
        return wins[kv].at[g, pl.ds(start, size), :]

    def own(g, kv, first=0, rows=2 * BLK):
        return hbms[kv].at[pl.ds(first, rows), columns(g)]

    def q_copy(g):
        cols = pl.ds(pl.multiple_of(g * GROUP * HD, GROUP * HD), GROUP * HD)
        return pltpu.make_async_copy(q_hbm.at[:, cols], q_buf.at[g], q_sem)

    def own_copy(g, kv):
        return pltpu.make_async_copy(own(g, kv), window(kv, g, 0), own_sem)

    def remote(src, dst, send, recv, to):
        return pltpu.make_async_remote_copy(
            src_ref=src, dst_ref=dst, send_sem=send, recv_sem=recv,
            device_id={"ctx": to}, device_id_type=MESH,
        )

    def settle(at, rows):
        part = k_win.at[:, pl.ds(0, rows), :]
        return remote(part, part, at, at, me)

    def odd_main(g, kv):
        return remote(own(g, kv), window(kv, g, 2), main_send, main_recv.at[g, kv], me + 2)

    def even_main(g, kv):
        return remote(
            own(g, kv, BLK, BLK), window(kv, g, 3), main_send, half_recv.at[g, kv], me + 3
        )

    def even_side(g, kv):
        return remote(
            own(g, kv, 0, BLK), wins[kv].at[g, pl.ds(BLK, BLK), :],
            main_send, main_recv.at[g, kv], me + 2,
        )

    def odd_side(g, kv):
        return remote(
            own(g, kv, BLK, BLK), window(kv, g, 3), side_send, side_recv.at[g, kv], me + 3
        )

    def even_near(g, kv):
        return remote(own(g, kv), window(kv, g, 1), near_send, side_recv.at[0, 0], me + 1)

    def odd_near(g, kv):
        return remote(
            wins[kv].at[g, pl.ds(0, 3 * BLK), :], wins[kv].at[g, pl.ds(2 * BLK, 3 * BLK), :],
            near_send, half_recv.at[g, kv], me - 1,
        )

    def hand(at):
        return remote(
            own(*relayed[at]), passing.at[at], main_send, pass_recv.at[at], me - 2
        )

    def pass_odd(at):
        g, kv = relayed[at]
        return remote(
            passing.at[at], window(kv, g, 2), pass_send, main_recv.at[g, kv], me + 4
        )

    def flag_odd():
        return remote(flags_out, flags_in.at[1], far_flag, flag_recv.at[1], me + 2)

    def flag_even():
        return remote(flags_out, flags_in.at[2], far_flag, flag_recv.at[2], me + 3)

    def flag_near():
        return remote(flags_out, flags_in.at[0], near_flag, flag_recv.at[0], me + 1)

    def flag_back():
        return remote(
            flags_in.at[pl.ds(1, 2)], flags_in.at[pl.ds(0, 2)], near_flag, flag_recv.at[0], me - 1
        )

    barrier = pltpu.get_barrier_semaphore()

    def signal(there, step):
        @pl.when(there)
        def _():
            pl.semaphore_signal(barrier, inc=1, device_id={"ctx": me + step}, device_id_type=MESH)

    signal(odd & prev, -2)
    signal(odd & prev, -3)
    signal(odd, -1)
    signal(odd & after2, 4)
    signal(even, 1)
    signal(odd & after, 2)
    heard = [
        (odd, 1), (odd & after, 1), (odd & prev, 1), (odd & prev2, 1), (even, 1), (even & after, 1),
    ]
    count = jnp.int32(0)
    for there, amount in heard:
        count = count + jnp.where(there, amount, 0)

    flag_copy = pltpu.make_async_copy(flags_hbm, flags_ref, flag_sem)
    flag_copy.start()
    for g, kv in PIECES:
        own_copy(g, kv).start()
        if kv == 0:
            q_copy(g).start()

    def blank(there, back):
        @pl.when(there)
        def _():
            start, size = ROWS[back]
            for win in wins:
                win[:, start:start + size, :] = jnp.zeros((KVH, size, HD), jnp.bfloat16)
            if back < 3:
                flags_in[back - 1] = jnp.zeros((8, BLK), jnp.int32)

    def when_direct(there, piece):
        return there & jnp.logical_not(hands) if piece in relayed else there

    flag_copy.wait()
    flags_out[0:1, :] = jnp.full((1, BLK), flags_ref[0], jnp.int32)
    flags_out[1:2, :] = jnp.full((1, BLK), flags_ref[1], jnp.int32)
    flags_out[2:8, :] = jnp.zeros((6, BLK), jnp.int32)
    pl.semaphore_wait(barrier, count)

    @pl.when(odd & after)
    def _():
        flag_odd().start()

    @pl.when(even & after)
    def _():
        flag_even().start()

    @pl.when(odd & prev)
    def _():
        pl.semaphore_signal(ready.at[0], inc=1, device_id={"ctx": me - 2}, device_id_type=MESH)

    @pl.when(odd & prev2)
    def _():
        pl.semaphore_signal(ready.at[1], inc=1, device_id={"ctx": me - 4}, device_id_type=MESH)

    @pl.when(even)
    def _():
        flag_near().start()

    for piece in PIECES[:ODD_LEAD]:
        @pl.when(when_direct(odd & after, piece))
        def _():
            odd_main(*piece).start()

    for piece in PIECES[:EVEN_LEAD]:
        @pl.when(even & after)
        def _():
            even_main(*piece).start()

    for at in range(len(relayed)):
        @pl.when(hands)
        def _():
            hand(at).start()

    @pl.when(even)
    def _():
        for piece in PIECES:
            even_near(*piece).start()

    @pl.when(odd & after)
    def _():
        pl.semaphore_wait(ready.at[0], 1)
        pl.semaphore_signal(ready.at[0], inc=1, device_id={"ctx": me - 1}, device_id_type=MESH)

    @pl.when(even & after)
    def _():
        pl.semaphore_wait(ready.at[0], 1)

    @pl.when(odd & after2)
    def _():
        pl.semaphore_wait(ready.at[1], 1)

    def far(piece):
        @pl.when(odd & after2)
        def _():
            odd_side(*piece).start()

    for at, piece in enumerate(PIECES):
        @pl.when(even & after)
        def _():
            even_side(*piece).start()

        if at < LATE:
            far(piece)
        for later in PIECES[at + ODD_LEAD:at + ODD_LEAD + 1]:
            @pl.when(when_direct(odd & after, later))
            def _():
                odd_main(*later).start()

        for later in PIECES[at + EVEN_LEAD:at + EVEN_LEAD + 1]:
            @pl.when(even & after)
            def _():
                even_main(*later).start()

    for piece in PIECES[LATE:]:
        far(piece)

    first = jnp.logical_not(prev)
    blank(even & first, 1)
    blank(first, 2)
    blank(odd & first | even & jnp.logical_not(prev2), 3)

    def arrive_odd(g, kv):
        @pl.when(odd & prev)
        def _():
            odd_main(g, kv).wait_recv()
            even_main(g, kv).wait_recv()
            odd_near(g, kv).start()

    def arrive_even(g, kv):
        @pl.when(even & prev)
        def _():
            odd_near(g, kv).wait_recv()
            even_side(g, kv).wait_recv()

    def arrive(g, kv):
        arrive_odd(g, kv)
        arrive_even(g, kv)

    def arrive_far(g, kv):
        @pl.when(even & prev2)
        def _():
            odd_side(g, kv).wait_recv()

    def pass_on(at):
        @pl.when(passes)
        def _():
            hand(at).wait_recv()
            pass_odd(at).start()

    @pl.when(odd & prev)
    def _():
        flag_odd().wait_recv()
        flag_even().wait_recv()
        flag_back().start()

    @pl.when(odd)
    def _():
        flag_near().wait_recv()
        settle(side_recv.at[0, 0], 4 * BLK).wait_recv()

    @pl.when(even & prev)
    def _():
        flag_back().wait_recv()

    pltpu.make_async_copy(q_hbm, q_hbm, q_sem).wait()
    own_part = k_win.at[:, pl.ds(0, 4 * BLK), :]
    pltpu.make_async_copy(own_part, own_part, own_sem).wait()

    mine = flags_out[...]
    begins = {0: mine[0:1], 1: mine[1:2]}
    for back in (1, 2):
        got = flags_in[back - 1]
        begins[-2 * back], begins[1 - 2 * back] = got[0:1], got[1:2]
    key_at = lax.broadcasted_iota(jnp.int32, (BLK, BLK), 0)
    row_at = lax.broadcasted_iota(jnp.int32, (BLK, BLK), 1)
    causal = jnp.where(key_at <= row_at, 0.0, NEG_FILL).astype(jnp.bfloat16)
    for i in range(2):
        bias[i, BACK * BLK:(BACK + 1) * BLK, :] = causal
        hidden = jnp.zeros((1, BLK), jnp.float32)
        for b in range(i - 1, i - BACK - 1, -1):
            hidden = jnp.where(begins[b + 1] != 0, NEG_FILL, hidden)
            at = (b - i + BACK) * BLK
            bias[i, at:at + BLK, :] = jnp.broadcast_to(hidden, (BLK, BLK)).astype(jnp.bfloat16)

    def scores(i, g, s_ref):
        s_ref[...] = score(i, q_buf.at[g], k_win.at[g], bias)

    def scores_and_weigh(i, g, s_ref, from_ref, w_ref):
        for rows, heads in PARTS:
            w_ref[rows, :] = weigh(from_ref[rows, :])
            s_ref[rows, :] = score(i, q_buf.at[g], k_win.at[g], bias, heads)

    def passed(g):
        for at in range(len(relayed)):
            @pl.when(g == PASS_AT)
            def _():
                pass_on(at)

    arrive(0, 0)
    scores(1, 0, s_buf.at[1])

    def one_group(g, carry):
        arrive_far(g, 0)
        arrive(g, 1)
        passed(g)
        scores(0, g, s_buf.at[0])
        mix(1, weigh(s_buf[1]), v_win.at[g], o_buf.at[g])
        arrive_far(g, 1)
        arrive(g + 1, 0)
        scores(1, g + 1, s_buf.at[1])
        mix(0, weigh(s_buf[0]), v_win.at[g], o_buf.at[g])
        return carry

    lax.fori_loop(0, LAST, one_group, 0)
    arrive_far(LAST, 0)
    arrive_odd(LAST, 1)
    scores_and_weigh(0, LAST, s_buf.at[0], s_buf.at[1], w_last)
    arrive_even(LAST, 1)
    arrive_far(LAST, 1)

    @pl.when(after)
    def _():
        settle(main_send, 4 * BLK).wait_send()

    @pl.when(odd & after)
    def _():
        flag_odd().wait_send()

    @pl.when(even & after)
    def _():
        flag_even().wait_send()

    @pl.when(even)
    def _():
        flag_near().wait_send()
        settle(near_send, 4 * BLK).wait_send()

    @pl.when(odd & after2)
    def _():
        settle(side_send, 2 * BLK).wait_send()

    @pl.when(odd & prev)
    def _():
        flag_back().wait_send()
        settle(near_send, REACH).wait_send()

    @pl.when(passes)
    def _():
        for at in range(len(relayed)):
            part = passing.at[at]
            remote(part, part, pass_send, pass_send, me).wait_send()


def per_device(n, relayed, queries, keys, values, doc_flags):
    rows = queries.shape[0]
    dma = pltpu.SemaphoreType.DMA
    inputs = [
        pltpu.with_memory_space_constraint(x, pltpu.HBM)
        for x in (queries, keys, values, doc_flags)
    ]
    kept = max(1, len(relayed))
    staged = pl.pallas_call(
        functools.partial(kernel, n, relayed),
        out_shape=[
            pltpu.VMEM((LAST, rows, GROUP * HD), jnp.bfloat16),
            pltpu.VMEM((KVH, WINDOW, HD), jnp.bfloat16),
            pltpu.VMEM((GROUP * BLK, REACH), jnp.bfloat16),
            pltpu.VMEM((2, GROUP * BLK, REACH), jnp.float32),
        ],
        in_specs=[pl.BlockSpec(memory_space=pltpu.HBM)] * 4,
        out_specs=[pl.BlockSpec(memory_space=pltpu.VMEM)] * 4,
        scratch_shapes=[
            pltpu.VMEM((KVH, rows, GROUP * HD), jnp.bfloat16),
            pltpu.VMEM((KVH, WINDOW, HD), jnp.bfloat16),
            pltpu.VMEM((2, REACH, BLK), jnp.bfloat16),
            pltpu.VMEM((kept, rows, HD), jnp.bfloat16),
            pltpu.SMEM(doc_flags.shape, jnp.int32),
            pltpu.VMEM((8, BLK), jnp.int32),
            pltpu.VMEM((3, 8, BLK), jnp.int32),
            dma((SEMS,)),
            dma((KVH, 2)),
            dma((KVH, 2)),
            dma((KVH, 2)),
            dma((kept,)),
            dma((3,)),
            pltpu.SemaphoreType.REGULAR((2,)),
        ],
        compiler_params=pltpu.CompilerParams(
            collective_id=0, has_side_effects=True, vmem_limit_bytes=40 * 1024 * 1024
        ),
        name="window_attention",
    )(*inputs)
    return pl.pallas_call(
        last_kernel,
        out_shape=jax.ShapeDtypeStruct(queries.shape, jnp.bfloat16),
        in_specs=[pl.BlockSpec(memory_space=pltpu.VMEM)] * 4,
        out_specs=pl.BlockSpec(memory_space=pltpu.HBM),
        scratch_shapes=[
            pltpu.VMEM((rows, GROUP * HD), jnp.bfloat16),
            pltpu.VMEM((GROUP * BLK, REACH), jnp.bfloat16),
            dma((KVH + 1,)),
        ],
        compiler_params=pltpu.CompilerParams(vmem_limit_bytes=32 * 1024 * 1024),
        name="last_group",
    )(*staged)


def solution(mesh):
    spread = P(("groups", "ctx"), None)
    n = mesh.shape["ctx"]
    relayed = RELAYED if mesh.shape["groups"] == 2 else []
    return jax.shard_map(
        functools.partial(per_device, n, relayed),
        mesh=mesh,
        in_specs=(spread, spread, spread, P(("groups", "ctx"))),
        out_specs=spread,
        check_vma=False,
    )
```

```python
import functools
import math

import jax
import jax.numpy as jnp
from jax import lax
from jax.experimental import pallas as pl
from jax.experimental.pallas import tpu as pltpu
from jax.sharding import PartitionSpec as P

HD = 128
KVH = 4
GROUP = 8
BLK = 128
BACK = 5
NEG_FILL = -1e30
SCALE2 = math.log2(math.e) / math.sqrt(HD)
MESH = pl.DeviceIdType.MESH
LAST = KVH - 1
PIECES = [(g, kv) for g in range(KVH) for kv in range(2)]
RELAYED = [(LAST - 1, 1)]
LATE = 4
PASS_AT = 1
SEMS = 9
ODD_LEAD = 2
EVEN_LEAD = 1

ROWS = {3: (0, BLK), 2: (BLK, 2 * BLK), 1: (3 * BLK, 2 * BLK), 0: (5 * BLK, 2 * BLK)}
WINDOW = 7 * BLK
REACH = 6 * BLK

HEADS = [pl.ds(j * HD, HD) for j in range(GROUP)]
STEP = 4
PARTS = [
    (pl.ds(j * BLK, STEP * BLK), HEADS[j:j + STEP]) for j in range(0, GROUP, STEP)
]


def score(i, q_ref, k_ref, bias, heads=HEADS):
    rows, keys = pl.ds(i * BLK, BLK), pl.ds(i * BLK, REACH)
    key_at = lax.broadcasted_iota(jnp.int32, (BLK, BLK), 0)
    row_at = lax.broadcasted_iota(jnp.int32, (BLK, BLK), 1)
    eye = (key_at == row_at).astype(jnp.bfloat16)
    q = jnp.concatenate(
        [jnp.concatenate([q_ref[rows, head], eye], axis=1) for head in heads], axis=0
    )
    k = jnp.concatenate([k_ref[keys, :], bias[i]], axis=1)
    return lax.dot_general(q, k, (((1,), (1,)), ((), ())), preferred_element_type=jnp.float32)


def weigh(s):
    top = jnp.max(s, axis=1, keepdims=True) * SCALE2
    return jnp.exp2(s * SCALE2 - top).astype(jnp.bfloat16)


def mix(i, w, v_ref, o_ref, heads=HEADS):
    v = jnp.concatenate(
        [v_ref[pl.ds(i * BLK, REACH), :], jnp.ones((REACH, HD), jnp.bfloat16)], axis=1
    )
    both = jnp.dot(w, v, preferred_element_type=jnp.float32)
    out = (both[:, :HD] / both[:, HD:]).astype(jnp.bfloat16)
    for j, head in enumerate(heads):
        o_ref[pl.ds(i * BLK, BLK), head] = out[j * BLK:(j + 1) * BLK]


def weigh_and_mix(s_ref, w_ref, i, mix_ref, v_ref, o_ref):
    for rows, heads in PARTS:
        w_ref[rows, :] = weigh(s_ref[rows, :])
        mix(i, mix_ref[rows, :], v_ref, o_ref, heads)


def last_kernel(o_first, v_win, w_last, s_last, o_hbm, o_buf, w_first, sem):
    width = GROUP * HD
    moves = []
    for g in range(LAST):
        move = pltpu.make_async_copy(
            o_first.at[g], o_hbm.at[:, pl.ds(g * width, width)], sem.at[g]
        )
        move.start()
        moves.append(move)
    for i in (1, 0):
        if i:
            weigh_and_mix(s_last.at[0], w_first, 1, w_last, v_win.at[LAST], o_buf)
        else:
            mix(0, w_first[...], v_win.at[LAST], o_buf)
        rows = pl.ds(i * BLK, BLK)
        move = pltpu.make_async_copy(
            o_buf.at[rows, :], o_hbm.at[rows, pl.ds(LAST * width, width)], sem.at[LAST + i]
        )
        move.start()
        moves.append(move)
    for move in moves:
        move.wait()


def kernel(
    n, relayed, q_hbm, k_hbm, v_hbm, flags_hbm,
    o_buf, v_win, w_last, s_buf,
    q_buf, k_win, bias, passing, flags_ref, flags_out, flags_in,
    sem, main_recv, half_recv, side_recv, pass_recv, flag_recv, ready,
):
    me = lax.axis_index("ctx")
    even, odd = lax.rem(me, 2) == 0, lax.rem(me, 2) == 1
    place = lax.rem(me, 4)
    prev, prev2 = me >= 2, me >= 4
    after, after2 = me + 2 < n, me + 4 < n
    hands = (place == 3) & after & bool(relayed)
    passes = (place == 1) & after2 & bool(relayed)

    wins, hbms = (k_win, v_win), (k_hbm, v_hbm)
    q_sem, own_sem, flag_sem, main_send, side_send, near_send, pass_send, near_flag, far_flag = (
        sem.at[at] for at in range(SEMS)
    )

    def columns(g):
        return pl.ds(pl.multiple_of(g * HD, HD), HD)

    def window(kv, g, back):
        start, size = ROWS[back]
        return wins[kv].at[g, pl.ds(start, size), :]

    def own(g, kv, first=0, rows=2 * BLK):
        return hbms[kv].at[pl.ds(first, rows), columns(g)]

    def q_copy(g):
        cols = pl.ds(pl.multiple_of(g * GROUP * HD, GROUP * HD), GROUP * HD)
        return pltpu.make_async_copy(q_hbm.at[:, cols], q_buf.at[g], q_sem)

    def own_copy(g, kv):
        return pltpu.make_async_copy(own(g, kv), window(kv, g, 0), own_sem)

    def remote(src, dst, send, recv, to):
        return pltpu.make_async_remote_copy(
            src_ref=src, dst_ref=dst, send_sem=send, recv_sem=recv,
            device_id={"ctx": to}, device_id_type=MESH,
        )

    def settle(at, rows):
        part = k_win.at[:, pl.ds(0, rows), :]
        return remote(part, part, at, at, me)

    def odd_main(g, kv):
        return remote(own(g, kv), window(kv, g, 2), main_send, main_recv.at[g, kv], me + 2)

    def even_main(g, kv):
        return remote(
            own(g, kv, BLK, BLK), window(kv, g, 3), main_send, half_recv.at[g, kv], me + 3
        )

    def even_side(g, kv):
        return remote(
            own(g, kv, 0, BLK), wins[kv].at[g, pl.ds(BLK, BLK), :],
            main_send, main_recv.at[g, kv], me + 2,
        )

    def odd_side(g, kv):
        return remote(
            own(g, kv, BLK, BLK), window(kv, g, 3), side_send, side_recv.at[g, kv], me + 3
        )

    def even_near(g, kv):
        return remote(own(g, kv), window(kv, g, 1), near_send, side_recv.at[0, 0], me + 1)

    def odd_near(g, kv):
        return remote(
            wins[kv].at[g, pl.ds(0, 3 * BLK), :], wins[kv].at[g, pl.ds(2 * BLK, 3 * BLK), :],
            near_send, half_recv.at[g, kv], me - 1,
        )

    def hand(at):
        return remote(
            own(*relayed[at]), passing.at[at], main_send, pass_recv.at[at], me - 2
        )

    def pass_odd(at):
        g, kv = relayed[at]
        return remote(
            passing.at[at], window(kv, g, 2), pass_send, main_recv.at[g, kv], me + 4
        )

    def flag_odd():
        return remote(flags_out, flags_in.at[1], far_flag, flag_recv.at[1], me + 2)

    def flag_even():
        return remote(flags_out, flags_in.at[2], far_flag, flag_recv.at[2], me + 3)

    def flag_near():
        return remote(flags_out, flags_in.at[0], near_flag, flag_recv.at[0], me + 1)

    def flag_back():
        return remote(
            flags_in.at[pl.ds(1, 2)], flags_in.at[pl.ds(0, 2)], near_flag, flag_recv.at[0], me - 1
        )

    barrier = pltpu.get_barrier_semaphore()

    def signal(there, step):
        @pl.when(there)
        def _():
            pl.semaphore_signal(barrier, inc=1, device_id={"ctx": me + step}, device_id_type=MESH)

    signal(odd & prev, -2)
    signal(odd & prev, -3)
    signal(odd, -1)
    signal(odd & after2, 4)
    signal(even, 1)
    signal(odd & after, 2)
    heard = [
        (odd, 1), (odd & after, 1), (odd & prev, 1), (odd & prev2, 1), (even, 1), (even & after, 1),
    ]
    count = jnp.int32(0)
    for there, amount in heard:
        count = count + jnp.where(there, amount, 0)

    flag_copy = pltpu.make_async_copy(flags_hbm, flags_ref, flag_sem)
    flag_copy.start()
    for g, kv in PIECES:
        own_copy(g, kv).start()
        if kv == 0:
            q_copy(g).start()

    def blank(there, back):
        @pl.when(there)
        def _():
            start, size = ROWS[back]
            for win in wins:
                win[:, start:start + size, :] = jnp.zeros((KVH, size, HD), jnp.bfloat16)
            if back < 3:
                flags_in[back - 1] = jnp.zeros((8, BLK), jnp.int32)

    def when_direct(there, piece):
        return there & jnp.logical_not(hands) if piece in relayed else there

    flag_copy.wait()
    flags_out[0:1, :] = jnp.full((1, BLK), flags_ref[0], jnp.int32)
    flags_out[1:2, :] = jnp.full((1, BLK), flags_ref[1], jnp.int32)
    flags_out[2:8, :] = jnp.zeros((6, BLK), jnp.int32)
    pl.semaphore_wait(barrier, count)

    @pl.when(odd & after)
    def _():
        flag_odd().start()

    @pl.when(even & after)
    def _():
        flag_even().start()

    @pl.when(odd & prev)
    def _():
        pl.semaphore_signal(ready.at[0], inc=1, device_id={"ctx": me - 2}, device_id_type=MESH)

    @pl.when(odd & prev2)
    def _():
        pl.semaphore_signal(ready.at[1], inc=1, device_id={"ctx": me - 4}, device_id_type=MESH)

    @pl.when(even)
    def _():
        flag_near().start()

    for piece in PIECES[:ODD_LEAD]:
        @pl.when(when_direct(odd & after, piece))
        def _():
            odd_main(*piece).start()

    for piece in PIECES[:EVEN_LEAD]:
        @pl.when(even & after)
        def _():
            even_main(*piece).start()

    for at in range(len(relayed)):
        @pl.when(hands)
        def _():
            hand(at).start()

    @pl.when(even)
    def _():
        for piece in PIECES:
            even_near(*piece).start()

    @pl.when(odd & after)
    def _():
        pl.semaphore_wait(ready.at[0], 1)
        pl.semaphore_signal(ready.at[0], inc=1, device_id={"ctx": me - 1}, device_id_type=MESH)

    @pl.when(even & after)
    def _():
        pl.semaphore_wait(ready.at[0], 1)

    @pl.when(odd & after2)
    def _():
        pl.semaphore_wait(ready.at[1], 1)

    def far(piece):
        @pl.when(odd & after2)
        def _():
            odd_side(*piece).start()

    for at, piece in enumerate(PIECES):
        @pl.when(even & after)
        def _():
            even_side(*piece).start()

        if at < LATE:
            far(piece)
        for later in PIECES[at + ODD_LEAD:at + ODD_LEAD + 1]:
            @pl.when(when_direct(odd & after, later))
            def _():
                odd_main(*later).start()

        for later in PIECES[at + EVEN_LEAD:at + EVEN_LEAD + 1]:
            @pl.when(even & after)
            def _():
                even_main(*later).start()

    for piece in PIECES[LATE:]:
        far(piece)

    first = jnp.logical_not(prev)
    blank(even & first, 1)
    blank(first, 2)
    blank(odd & first | even & jnp.logical_not(prev2), 3)

    def arrive_odd(g, kv):
        @pl.when(odd & prev)
        def _():
            odd_main(g, kv).wait_recv()
            even_main(g, kv).wait_recv()
            odd_near(g, kv).start()

    def arrive_even(g, kv):
        @pl.when(even & prev)
        def _():
            odd_near(g, kv).wait_recv()
            even_side(g, kv).wait_recv()

    def arrive(g, kv):
        arrive_odd(g, kv)
        arrive_even(g, kv)

    def arrive_far(g, kv):
        @pl.when(even & prev2)
        def _():
            odd_side(g, kv).wait_recv()

    def pass_on(at):
        @pl.when(passes)
        def _():
            hand(at).wait_recv()
            pass_odd(at).start()

    @pl.when(odd & prev)
    def _():
        flag_odd().wait_recv()
        flag_even().wait_recv()
        flag_back().start()

    @pl.when(odd)
    def _():
        flag_near().wait_recv()
        settle(side_recv.at[0, 0], 4 * BLK).wait_recv()

    @pl.when(even & prev)
    def _():
        flag_back().wait_recv()

    pltpu.make_async_copy(q_hbm, q_hbm, q_sem).wait()
    own_part = k_win.at[:, pl.ds(0, 4 * BLK), :]
    pltpu.make_async_copy(own_part, own_part, own_sem).wait()

    mine = flags_out[...]
    begins = {0: mine[0:1], 1: mine[1:2]}
    for back in (1, 2):
        got = flags_in[back - 1]
        begins[-2 * back], begins[1 - 2 * back] = got[0:1], got[1:2]
    key_at = lax.broadcasted_iota(jnp.int32, (BLK, BLK), 0)
    row_at = lax.broadcasted_iota(jnp.int32, (BLK, BLK), 1)
    causal = jnp.where(key_at <= row_at, 0.0, NEG_FILL).astype(jnp.bfloat16)
    for i in range(2):
        bias[i, BACK * BLK:(BACK + 1) * BLK, :] = causal
        hidden = jnp.zeros((1, BLK), jnp.float32)
        for b in range(i - 1, i - BACK - 1, -1):
            hidden = jnp.where(begins[b + 1] != 0, NEG_FILL, hidden)
            at = (b - i + BACK) * BLK
            bias[i, at:at + BLK, :] = jnp.broadcast_to(hidden, (BLK, BLK)).astype(jnp.bfloat16)

    def scores(i, g, s_ref):
        s_ref[...] = score(i, q_buf.at[g], k_win.at[g], bias)

    def scores_and_weigh(i, g, s_ref, from_ref, w_ref):
        for rows, heads in PARTS:
            w_ref[rows, :] = weigh(from_ref[rows, :])
            s_ref[rows, :] = score(i, q_buf.at[g], k_win.at[g], bias, heads)

    def passed(g):
        for at in range(len(relayed)):
            @pl.when(g == PASS_AT)
            def _():
                pass_on(at)

    arrive(0, 0)
    scores(1, 0, s_buf.at[1])

    def one_group(g, carry):
        arrive_far(g, 0)
        arrive(g, 1)
        passed(g)
        scores(0, g, s_buf.at[0])
        mix(1, weigh(s_buf[1]), v_win.at[g], o_buf.at[g])
        arrive_far(g, 1)
        arrive(g + 1, 0)
        scores(1, g + 1, s_buf.at[1])
        mix(0, weigh(s_buf[0]), v_win.at[g], o_buf.at[g])
        return carry

    waits_far = (place == 2) & prev2
    split = jnp.where(waits_far, LAST - 1, LAST)
    lax.fori_loop(0, split, one_group, 0)

    def late_group(g, carry):
        arrive_even(g, 1)
        mix(1, weigh(s_buf[1]), v_win.at[g], o_buf.at[g])
        arrive_even(g + 1, 0)
        scores(1, g + 1, s_buf.at[0])
        w_last[...] = weigh(s_buf[0])
        arrive_far(g, 0)
        scores(0, g, s_buf.at[1])
        arrive_far(g, 1)
        arrive_far(g + 1, 0)
        scores(0, g + 1, s_buf.at[0])
        mix(0, weigh(s_buf[1]), v_win.at[g], o_buf.at[g])
        return carry

    lax.fori_loop(split, LAST, late_group, 0)

    @pl.when(jnp.logical_not(waits_far))
    def _():
        arrive_far(LAST, 0)
        arrive_odd(LAST, 1)
        scores_and_weigh(0, LAST, s_buf.at[0], s_buf.at[1], w_last)

    arrive_even(LAST, 1)
    arrive_far(LAST, 1)

    @pl.when(after)
    def _():
        settle(main_send, 4 * BLK).wait_send()

    @pl.when(odd & after)
    def _():
        flag_odd().wait_send()

    @pl.when(even & after)
    def _():
        flag_even().wait_send()

    @pl.when(even)
    def _():
        flag_near().wait_send()
        settle(near_send, 4 * BLK).wait_send()

    @pl.when(odd & after2)
    def _():
        settle(side_send, 2 * BLK).wait_send()

    @pl.when(odd & prev)
    def _():
        flag_back().wait_send()
        settle(near_send, REACH).wait_send()

    @pl.when(passes)
    def _():
        for at in range(len(relayed)):
            part = passing.at[at]
            remote(part, part, pass_send, pass_send, me).wait_send()


def per_device(n, relayed, queries, keys, values, doc_flags):
    rows = queries.shape[0]
    dma = pltpu.SemaphoreType.DMA
    inputs = [
        pltpu.with_memory_space_constraint(x, pltpu.HBM)
        for x in (queries, keys, values, doc_flags)
    ]
    kept = max(1, len(relayed))
    staged = pl.pallas_call(
        functools.partial(kernel, n, relayed),
        out_shape=[
            pltpu.VMEM((LAST, rows, GROUP * HD), jnp.bfloat16),
            pltpu.VMEM((KVH, WINDOW, HD), jnp.bfloat16),
            pltpu.VMEM((GROUP * BLK, REACH), jnp.bfloat16),
            pltpu.VMEM((2, GROUP * BLK, REACH), jnp.float32),
        ],
        in_specs=[pl.BlockSpec(memory_space=pltpu.HBM)] * 4,
        out_specs=[pl.BlockSpec(memory_space=pltpu.VMEM)] * 4,
        scratch_shapes=[
            pltpu.VMEM((KVH, rows, GROUP * HD), jnp.bfloat16),
            pltpu.VMEM((KVH, WINDOW, HD), jnp.bfloat16),
            pltpu.VMEM((2, REACH, BLK), jnp.bfloat16),
            pltpu.VMEM((kept, rows, HD), jnp.bfloat16),
            pltpu.SMEM(doc_flags.shape, jnp.int32),
            pltpu.VMEM((8, BLK), jnp.int32),
            pltpu.VMEM((3, 8, BLK), jnp.int32),
            dma((SEMS,)),
            dma((KVH, 2)),
            dma((KVH, 2)),
            dma((KVH, 2)),
            dma((kept,)),
            dma((3,)),
            pltpu.SemaphoreType.REGULAR((2,)),
        ],
        compiler_params=pltpu.CompilerParams(
            collective_id=0, has_side_effects=True, vmem_limit_bytes=40 * 1024 * 1024
        ),
        name="window_attention",
    )(*inputs)
    return pl.pallas_call(
        last_kernel,
        out_shape=jax.ShapeDtypeStruct(queries.shape, jnp.bfloat16),
        in_specs=[pl.BlockSpec(memory_space=pltpu.VMEM)] * 4,
        out_specs=pl.BlockSpec(memory_space=pltpu.HBM),
        scratch_shapes=[
            pltpu.VMEM((rows, GROUP * HD), jnp.bfloat16),
            pltpu.VMEM((GROUP * BLK, REACH), jnp.bfloat16),
            dma((KVH + 1,)),
        ],
        compiler_params=pltpu.CompilerParams(vmem_limit_bytes=32 * 1024 * 1024),
        name="last_group",
    )(*staged)


def solution(mesh):
    spread = P(("groups", "ctx"), None)
    n = mesh.shape["ctx"]
    relayed = RELAYED if mesh.shape["groups"] == 2 else []
    return jax.shard_map(
        functools.partial(per_device, n, relayed),
        mesh=mesh,
        in_specs=(spread, spread, spread, P(("groups", "ctx"))),
        out_specs=spread,
        check_vma=False,
    )
```

```python
import functools
import math

import jax
import jax.numpy as jnp
from jax import lax
from jax.experimental import pallas as pl
from jax.experimental.pallas import tpu as pltpu
from jax.sharding import PartitionSpec as P

HD = 128
KVH = 4
GROUP = 8
BLK = 128
BACK = 5
NEG_FILL = -1e30
SCALE2 = math.log2(math.e) / math.sqrt(HD)
MESH = pl.DeviceIdType.MESH
LAST = KVH - 1
PIECES = [(g, kv) for g in range(KVH) for kv in range(2)]
RELAYED = [(LAST - 1, 1)]
LATE = 4
PASS_AT = 1
SEMS = 9
ODD_LEAD = 2
EVEN_LEAD = 1

ROWS = {3: (0, BLK), 2: (BLK, 2 * BLK), 1: (3 * BLK, 2 * BLK), 0: (5 * BLK, 2 * BLK)}
WINDOW = 7 * BLK
REACH = 6 * BLK

HEADS = [pl.ds(j * HD, HD) for j in range(GROUP)]
STEP = 2
PARTS = [
    (pl.ds(j * BLK, STEP * BLK), HEADS[j:j + STEP]) for j in range(0, GROUP, STEP)
]


def score(i, q_ref, k_ref, bias, heads=HEADS):
    rows, keys = pl.ds(i * BLK, BLK), pl.ds(i * BLK, REACH)
    key_at = lax.broadcasted_iota(jnp.int32, (BLK, BLK), 0)
    row_at = lax.broadcasted_iota(jnp.int32, (BLK, BLK), 1)
    eye = (key_at == row_at).astype(jnp.bfloat16)
    q = jnp.concatenate(
        [jnp.concatenate([q_ref[rows, head], eye], axis=1) for head in heads], axis=0
    )
    k = jnp.concatenate([k_ref[keys, :], bias[i]], axis=1)
    return lax.dot_general(q, k, (((1,), (1,)), ((), ())), preferred_element_type=jnp.float32)


def weigh(s):
    top = jnp.max(s, axis=1, keepdims=True) * SCALE2
    return jnp.exp2(s * SCALE2 - top).astype(jnp.bfloat16)


def mix(i, w, v_ref, o_ref, heads=HEADS):
    v = jnp.concatenate(
        [v_ref[pl.ds(i * BLK, REACH), :], jnp.ones((REACH, HD), jnp.bfloat16)], axis=1
    )
    both = jnp.dot(w, v, preferred_element_type=jnp.float32)
    out = (both[:, :HD] / both[:, HD:]).astype(jnp.bfloat16)
    for j, head in enumerate(heads):
        o_ref[pl.ds(i * BLK, BLK), head] = out[j * BLK:(j + 1) * BLK]


def weigh_and_mix(s_ref, w_ref, i, mix_ref, v_ref, o_ref):
    for rows, heads in PARTS:
        w_ref[rows, :] = weigh(s_ref[rows, :])
        mix(i, mix_ref[rows, :], v_ref, o_ref, heads)


def last_kernel(o_first, v_win, w_last, s_last, o_hbm, o_buf, w_first, sem):
    width = GROUP * HD
    moves = []
    for g in range(LAST):
        move = pltpu.make_async_copy(
            o_first.at[g], o_hbm.at[:, pl.ds(g * width, width)], sem.at[g]
        )
        move.start()
        moves.append(move)
    for i in (1, 0):
        if i:
            weigh_and_mix(s_last.at[0], w_first, 1, w_last, v_win.at[LAST], o_buf)
        else:
            mix(0, w_first[...], v_win.at[LAST], o_buf)
        rows = pl.ds(i * BLK, BLK)
        move = pltpu.make_async_copy(
            o_buf.at[rows, :], o_hbm.at[rows, pl.ds(LAST * width, width)], sem.at[LAST + i]
        )
        move.start()
        moves.append(move)
    for move in moves:
        move.wait()


def kernel(
    n, relayed, q_hbm, k_hbm, v_hbm, flags_hbm,
    o_buf, v_win, w_last, s_buf,
    q_buf, k_win, bias, passing, flags_ref, flags_out, flags_in,
    sem, main_recv, side_recv, pass_recv, flag_recv, ready,
):
    me = lax.axis_index("ctx")
    even, odd = lax.rem(me, 2) == 0, lax.rem(me, 2) == 1
    place = lax.rem(me, 4)
    prev, prev2 = me >= 2, me >= 4
    after, after2 = me + 2 < n, me + 4 < n
    hands = (place == 3) & after & bool(relayed)
    passes = (place == 1) & after2 & bool(relayed)

    wins, hbms = (k_win, v_win), (k_hbm, v_hbm)
    q_sem, own_sem, flag_sem, main_send, side_send, near_send, pass_send, near_flag, far_flag = (
        sem.at[at] for at in range(SEMS)
    )

    def columns(g):
        return pl.ds(pl.multiple_of(g * HD, HD), HD)

    def window(kv, g, back):
        start, size = ROWS[back]
        return wins[kv].at[g, pl.ds(start, size), :]

    def own(g, kv, first=0, rows=2 * BLK):
        return hbms[kv].at[pl.ds(first, rows), columns(g)]

    def q_copy(g):
        cols = pl.ds(pl.multiple_of(g * GROUP * HD, GROUP * HD), GROUP * HD)
        return pltpu.make_async_copy(q_hbm.at[:, cols], q_buf.at[g], q_sem)

    def own_copy(g, kv):
        return pltpu.make_async_copy(own(g, kv), window(kv, g, 0), own_sem)

    def remote(src, dst, send, recv, to):
        return pltpu.make_async_remote_copy(
            src_ref=src, dst_ref=dst, send_sem=send, recv_sem=recv,
            device_id={"ctx": to}, device_id_type=MESH,
        )

    def settle(at, rows):
        part = k_win.at[:, pl.ds(0, rows), :]
        return remote(part, part, at, at, me)

    def odd_main(g, kv):
        return remote(own(g, kv), window(kv, g, 2), main_send, main_recv.at[g, kv], me + 2)

    def even_main(g, kv):
        return remote(
            own(g, kv, BLK, BLK), window(kv, g, 3), main_send, main_recv.at[g, kv], me + 3
        )

    def even_side(g, kv):
        return remote(
            own(g, kv, 0, BLK), wins[kv].at[g, pl.ds(BLK, BLK), :],
            main_send, main_recv.at[g, kv], me + 2,
        )

    def odd_side(g, kv):
        return remote(
            own(g, kv, BLK, BLK), window(kv, g, 3), side_send, side_recv.at[g, kv], me + 3
        )

    def even_near(g, kv):
        return remote(own(g, kv), window(kv, g, 1), near_send, side_recv.at[0, 0], me + 1)

    def odd_near(g, kv):
        return remote(
            wins[kv].at[g, pl.ds(0, 3 * BLK), :], wins[kv].at[g, pl.ds(2 * BLK, 3 * BLK), :],
            near_send, main_recv.at[g, kv], me - 1,
        )

    def hand(at):
        return remote(
            own(*relayed[at]), passing.at[at], main_send, pass_recv.at[at], me - 2
        )

    def pass_odd(at):
        g, kv = relayed[at]
        return remote(
            passing.at[at], window(kv, g, 2), pass_send, main_recv.at[g, kv], me + 4
        )

    def flag_odd():
        return remote(flags_out, flags_in.at[1], far_flag, flag_recv.at[1], me + 2)

    def flag_even():
        return remote(flags_out, flags_in.at[2], far_flag, flag_recv.at[2], me + 3)

    def flag_near():
        return remote(flags_out, flags_in.at[0], near_flag, flag_recv.at[0], me + 1)

    def flag_back():
        return remote(
            flags_in.at[pl.ds(1, 2)], flags_in.at[pl.ds(0, 2)], near_flag, flag_recv.at[0], me - 1
        )

    barrier = pltpu.get_barrier_semaphore()

    def signal(there, step):
        @pl.when(there)
        def _():
            pl.semaphore_signal(barrier, inc=1, device_id={"ctx": me + step}, device_id_type=MESH)

    signal(odd & prev, -2)
    signal(odd & prev, -3)
    signal(odd, -1)
    signal(odd & after2, 4)
    signal(even, 1)
    signal(odd & after, 2)
    heard = [
        (odd, 1), (odd & after, 1), (odd & prev, 1), (odd & prev2, 1), (even, 1), (even & after, 1),
    ]
    count = jnp.int32(0)
    for there, amount in heard:
        count = count + jnp.where(there, amount, 0)

    flag_copy = pltpu.make_async_copy(flags_hbm, flags_ref, flag_sem)
    flag_copy.start()
    for g, kv in PIECES:
        own_copy(g, kv).start()
        if kv == 0:
            q_copy(g).start()

    def blank(there, back):
        @pl.when(there)
        def _():
            start, size = ROWS[back]
            for win in wins:
                win[:, start:start + size, :] = jnp.zeros((KVH, size, HD), jnp.bfloat16)
            if back < 3:
                flags_in[back - 1] = jnp.zeros((8, BLK), jnp.int32)

    def when_direct(there, piece):
        return there & jnp.logical_not(hands) if piece in relayed else there

    flag_copy.wait()
    flags_out[0:1, :] = jnp.full((1, BLK), flags_ref[0], jnp.int32)
    flags_out[1:2, :] = jnp.full((1, BLK), flags_ref[1], jnp.int32)
    flags_out[2:8, :] = jnp.zeros((6, BLK), jnp.int32)
    pl.semaphore_wait(barrier, count)

    @pl.when(odd & after)
    def _():
        flag_odd().start()

    @pl.when(even & after)
    def _():
        flag_even().start()

    @pl.when(odd & prev)
    def _():
        pl.semaphore_signal(ready.at[0], inc=1, device_id={"ctx": me - 2}, device_id_type=MESH)

    @pl.when(odd & prev2)
    def _():
        pl.semaphore_signal(ready.at[1], inc=1, device_id={"ctx": me - 4}, device_id_type=MESH)

    @pl.when(even)
    def _():
        flag_near().start()

    for piece in PIECES[:ODD_LEAD]:
        @pl.when(when_direct(odd & after, piece))
        def _():
            odd_main(*piece).start()

    for piece in PIECES[:EVEN_LEAD]:
        @pl.when(even & after)
        def _():
            even_main(*piece).start()

    for at in range(len(relayed)):
        @pl.when(hands)
        def _():
            hand(at).start()

    @pl.when(even)
    def _():
        for piece in PIECES:
            even_near(*piece).start()

    @pl.when(odd & after)
    def _():
        pl.semaphore_wait(ready.at[0], 1)
        pl.semaphore_signal(ready.at[0], inc=1, device_id={"ctx": me - 1}, device_id_type=MESH)

    @pl.when(even & after)
    def _():
        pl.semaphore_wait(ready.at[0], 1)

    @pl.when(odd & after2)
    def _():
        pl.semaphore_wait(ready.at[1], 1)

    def far(piece):
        @pl.when(odd & after2)
        def _():
            odd_side(*piece).start()

    for at, piece in enumerate(PIECES):
        @pl.when(even & after)
        def _():
            even_side(*piece).start()

        if at < LATE:
            far(piece)
        for later in PIECES[at + ODD_LEAD:at + ODD_LEAD + 1]:
            @pl.when(when_direct(odd & after, later))
            def _():
                odd_main(*later).start()

        for later in PIECES[at + EVEN_LEAD:at + EVEN_LEAD + 1]:
            @pl.when(even & after)
            def _():
                even_main(*later).start()

    for piece in PIECES[LATE:]:
        far(piece)

    first = jnp.logical_not(prev)
    blank(even & first, 1)
    blank(first, 2)
    blank(odd & first | even & jnp.logical_not(prev2), 3)

    def landed(g, kv, start, rows):
        part = wins[kv].at[g, pl.ds(start, rows), :]
        remote(part, part, main_send, main_recv.at[g, kv], me).wait_recv()

    def arrive_odd(g, kv):
        @pl.when(odd & prev)
        def _():
            landed(g, kv, 0, 3 * BLK)
            odd_near(g, kv).start()

    def arrive_even(g, kv):
        @pl.when(even & prev)
        def _():
            landed(g, kv, BLK, 4 * BLK)

    def arrive(g, kv):
        arrive_odd(g, kv)
        arrive_even(g, kv)

    def arrive_far(g, kv):
        @pl.when(even & prev2)
        def _():
            odd_side(g, kv).wait_recv()

    def pass_on(at):
        @pl.when(passes)
        def _():
            hand(at).wait_recv()
            pass_odd(at).start()

    @pl.when(odd & prev)
    def _():
        flag_odd().wait_recv()
        flag_even().wait_recv()
        flag_back().start()

    @pl.when(odd)
    def _():
        flag_near().wait_recv()
        settle(side_recv.at[0, 0], 4 * BLK).wait_recv()

    @pl.when(even & prev)
    def _():
        flag_back().wait_recv()

    pltpu.make_async_copy(q_hbm, q_hbm, q_sem).wait()
    own_part = k_win.at[:, pl.ds(0, 4 * BLK), :]
    pltpu.make_async_copy(own_part, own_part, own_sem).wait()

    mine = flags_out[...]
    begins = {0: mine[0:1], 1: mine[1:2]}
    for back in (1, 2):
        got = flags_in[back - 1]
        begins[-2 * back], begins[1 - 2 * back] = got[0:1], got[1:2]
    key_at = lax.broadcasted_iota(jnp.int32, (BLK, BLK), 0)
    row_at = lax.broadcasted_iota(jnp.int32, (BLK, BLK), 1)
    causal = jnp.where(key_at <= row_at, 0.0, NEG_FILL).astype(jnp.bfloat16)
    for i in range(2):
        bias[i, BACK * BLK:(BACK + 1) * BLK, :] = causal
        hidden = jnp.zeros((1, BLK), jnp.float32)
        for b in range(i - 1, i - BACK - 1, -1):
            hidden = jnp.where(begins[b + 1] != 0, NEG_FILL, hidden)
            at = (b - i + BACK) * BLK
            bias[i, at:at + BLK, :] = jnp.broadcast_to(hidden, (BLK, BLK)).astype(jnp.bfloat16)

    def scores(i, g, s_ref):
        s_ref[...] = score(i, q_buf.at[g], k_win.at[g], bias)

    def scores_and_weigh(i, g, s_ref, from_ref, w_ref):
        for rows, heads in PARTS:
            w_ref[rows, :] = weigh(from_ref[rows, :])
            s_ref[rows, :] = score(i, q_buf.at[g], k_win.at[g], bias, heads)

    def passed(g):
        for at in range(len(relayed)):
            @pl.when(g == PASS_AT)
            def _():
                pass_on(at)

    arrive(0, 0)
    scores(1, 0, s_buf.at[1])

    def one_group(g, carry):
        arrive_far(g, 0)
        arrive(g, 1)
        passed(g)
        scores(0, g, s_buf.at[0])
        mix(1, weigh(s_buf[1]), v_win.at[g], o_buf.at[g])
        arrive_far(g, 1)
        arrive(g + 1, 0)
        scores(1, g + 1, s_buf.at[1])
        mix(0, weigh(s_buf[0]), v_win.at[g], o_buf.at[g])
        return carry

    waits_far = (place == 2) & prev2
    split = jnp.where(waits_far, LAST - 1, LAST)
    lax.fori_loop(0, split, one_group, 0)

    def late_group(g, carry):
        arrive_even(g, 1)
        mix(1, weigh(s_buf[1]), v_win.at[g], o_buf.at[g])
        arrive_even(g + 1, 0)
        scores(1, g + 1, s_buf.at[0])
        w_last[...] = weigh(s_buf[0])
        arrive_far(g, 0)
        scores(0, g, s_buf.at[1])
        arrive_far(g, 1)
        arrive_far(g + 1, 0)
        scores(0, g + 1, s_buf.at[0])
        mix(0, weigh(s_buf[1]), v_win.at[g], o_buf.at[g])
        return carry

    lax.fori_loop(split, LAST, late_group, 0)

    @pl.when(jnp.logical_not(waits_far))
    def _():
        arrive_far(LAST, 0)
        arrive_odd(LAST, 1)
        scores_and_weigh(0, LAST, s_buf.at[0], s_buf.at[1], w_last)

    arrive_even(LAST, 1)
    arrive_far(LAST, 1)

    @pl.when(after)
    def _():
        settle(main_send, 4 * BLK).wait_send()

    @pl.when(odd & after)
    def _():
        flag_odd().wait_send()

    @pl.when(even & after)
    def _():
        flag_even().wait_send()

    @pl.when(even)
    def _():
        flag_near().wait_send()
        settle(near_send, 4 * BLK).wait_send()

    @pl.when(odd & after2)
    def _():
        settle(side_send, 2 * BLK).wait_send()

    @pl.when(odd & prev)
    def _():
        flag_back().wait_send()
        settle(near_send, REACH).wait_send()

    @pl.when(passes)
    def _():
        for at in range(len(relayed)):
            part = passing.at[at]
            remote(part, part, pass_send, pass_send, me).wait_send()


def per_device(n, relayed, queries, keys, values, doc_flags):
    rows = queries.shape[0]
    dma = pltpu.SemaphoreType.DMA
    inputs = [
        pltpu.with_memory_space_constraint(x, pltpu.HBM)
        for x in (queries, keys, values, doc_flags)
    ]
    kept = max(1, len(relayed))
    staged = pl.pallas_call(
        functools.partial(kernel, n, relayed),
        out_shape=[
            pltpu.VMEM((LAST, rows, GROUP * HD), jnp.bfloat16),
            pltpu.VMEM((KVH, WINDOW, HD), jnp.bfloat16),
            pltpu.VMEM((GROUP * BLK, REACH), jnp.bfloat16),
            pltpu.VMEM((2, GROUP * BLK, REACH), jnp.float32),
        ],
        in_specs=[pl.BlockSpec(memory_space=pltpu.HBM)] * 4,
        out_specs=[pl.BlockSpec(memory_space=pltpu.VMEM)] * 4,
        scratch_shapes=[
            pltpu.VMEM((KVH, rows, GROUP * HD), jnp.bfloat16),
            pltpu.VMEM((KVH, WINDOW, HD), jnp.bfloat16),
            pltpu.VMEM((2, REACH, BLK), jnp.bfloat16),
            pltpu.VMEM((kept, rows, HD), jnp.bfloat16),
            pltpu.SMEM(doc_flags.shape, jnp.int32),
            pltpu.VMEM((8, BLK), jnp.int32),
            pltpu.VMEM((3, 8, BLK), jnp.int32),
            dma((SEMS,)),
            dma((KVH, 2)),
            dma((KVH, 2)),
            dma((kept,)),
            dma((3,)),
            pltpu.SemaphoreType.REGULAR((2,)),
        ],
        compiler_params=pltpu.CompilerParams(
            collective_id=0, has_side_effects=True, vmem_limit_bytes=40 * 1024 * 1024
        ),
        name="window_attention",
    )(*inputs)
    return pl.pallas_call(
        last_kernel,
        out_shape=jax.ShapeDtypeStruct(queries.shape, jnp.bfloat16),
        in_specs=[pl.BlockSpec(memory_space=pltpu.VMEM)] * 4,
        out_specs=pl.BlockSpec(memory_space=pltpu.HBM),
        scratch_shapes=[
            pltpu.VMEM((rows, GROUP * HD), jnp.bfloat16),
            pltpu.VMEM((GROUP * BLK, REACH), jnp.bfloat16),
            dma((KVH + 1,)),
        ],
        compiler_params=pltpu.CompilerParams(vmem_limit_bytes=32 * 1024 * 1024),
        name="last_group",
    )(*staged)


def solution(mesh):
    spread = P(("groups", "ctx"), None)
    n = mesh.shape["ctx"]
    relayed = RELAYED if mesh.shape["groups"] == 2 else []
    return jax.shard_map(
        functools.partial(per_device, n, relayed),
        mesh=mesh,
        in_specs=(spread, spread, spread, P(("groups", "ctx"))),
        out_specs=spread,
        check_vma=False,
    )
```
